512 devices in a mesh: section: 64 (over y, x, core), dp: 8 (over z).
Axes of the slice: x: 4, y: 8, z: 8, core: 2. Of those that a mesh axis runs over, the one named last changes fastest.
Arguments:
- cotangent: bfloat16 [512, 8192], P('dp'), may hold values from -96 to 96
- lengths: int32 [16], P('dp'), may hold values from 1 to 32, as said below
- example_ids: int32 [512], P('dp'), may hold values from -1 to 15, as said below
- layer_inputs: bfloat16 [512, 32768], P('dp', 'section'), may hold values from -6 to 6
- preacts: bfloat16 [512, 32768], P('dp', 'section'), may hold values from -6 to 6
- weights: bfloat16 [32768, 8192], P('section', 'dp'), may hold values from -0.0625 to 0.0625
- query_left: bfloat16 [32768, 256], P('section'), may hold values from -0.0625 to 0.0625
- query_right: bfloat16 [32768, 256], P('section'), may hold values from -0.0625 to 0.0625
Outputs:
- input_grads: bfloat16 [512, 32768], P('dp', 'section')
- scores: float32 [16, 16], P('dp')
The draws below stay inside these ranges and needn't reach their ends.
Inputs may be any that keep to these rules, and one draw needn't show every extreme that they name: In each aligned block of 2 sequences one length is exactly 32; the lengths of a block sum to at most 64. `example_ids`: rows n * 64 to (n + 1) * 64 - 1 hold sequences n * 2 to (n + 1) * 2 - 1 in order from the block's first row, each on as many consecutive rows as its length; the block's remaining rows hold -1.
All inputs are finite; a program needn't handle non-finite values.
Results may differ from the reference program's by a relative error of at most 0.0066.
Values may be sent and summed in bfloat16 or wider, within the bound.
A program may use at most 64 MiB of HBM per device.

```python
import jax
import jax.numpy as jnp
from jax import lax

D = 8192
LAYERS = 4
QUERIES = 16
RANK = 16
TOK_DEV = 64
SEQ_DEV = 2
QK = 256
MAXLEN = 32
SEQS = 16
TOKENS = 512


def packing(key):
    groups = SEQS // SEQ_DEV
    divisor_bits = jax.random.bits(jax.random.fold_in(key, 4101), (groups, SEQ_DEV), jnp.uint32)
    chosen_bits = jax.random.bits(jax.random.fold_in(key, 4207), (groups, 1), jnp.uint32)
    divisor = (divisor_bits % 6).astype(jnp.int32) + 1
    chosen = (chosen_bits % SEQ_DEV).astype(jnp.int32)
    spans = jnp.maximum(MAXLEN // divisor, 1)
    slot_ids = jnp.arange(SEQ_DEV, dtype=jnp.int32)[None, :]
    spans = jnp.where(slot_ids == chosen, MAXLEN, spans).astype(jnp.int32)
    run_ends = jnp.cumsum(spans, axis=1)
    row_ids = jnp.arange(TOK_DEV, dtype=jnp.int32)
    before = jnp.sum((row_ids[None, :, None] >= run_ends[:, None, :]).astype(jnp.int32), axis=2)
    live_total = run_ends[:, -1:]
    owners = jnp.arange(groups, dtype=jnp.int32)[:, None] * SEQ_DEV + before
    token_ids = jnp.where(row_ids[None, :] < live_total, owners, -1)
    return (spans.reshape(SEQS).astype(jnp.int32), token_ids.reshape(TOKENS).astype(jnp.int32))


def draw_lengths(key, part):
    return packing(key)[0]


def draw_example_ids(key, part):
    return packing(key)[1]


def steps_of(own_key, dims, shards, smallest, high):
    gain, own = 1.0, jax.random.fold_in(own_key, 6)
    for position, parts in shards:
        steps = jnp.exp(jax.random.uniform(jax.random.fold_in(own, position), (parts,), jnp.float32, smallest / len(shards), high / len(shards)))
        gain = gain * jnp.repeat(steps, dims[position] // parts).reshape([-1 if axis == position else 1 for axis in range(len(dims))])
    return gain


def scatter_about(own_key, shape, deviation, limit, split=(), kind=jnp.bfloat16):
    array = jax.random.normal(own_key, shape, jnp.float32) * deviation
    if len(split) > 0:
        array = steps_of(own_key, shape, split, -0.22, 0.18) * array
    return jnp.clip(array, min=-limit, max=limit).astype(kind)


def setup_inputs(seed: int = 0) -> dict:
    streams_of = jax.random.split(jax.random.key(seed), 9)
    cotangent = scatter_about(streams_of[0], (TOKENS, D), (MAXLEN // 2), 96.0, ((0, 8),))
    lengths = draw_lengths(jax.random.fold_in(streams_of[8], 71), 0)
    example_ids = draw_example_ids(jax.random.fold_in(streams_of[8], 71), 0)
    layer_inputs = scatter_about(streams_of[3], (TOKENS, LAYERS * D), 1.0, 6.0, ((0, 8), (1, 64)))
    preacts = scatter_about(streams_of[4], (TOKENS, LAYERS * D), 1.0, 6.0, ((0, 8), (1, 64)))
    weights = scatter_about(streams_of[5], (LAYERS * D, D), D ** -0.5, 0.0625, ((0, 64), (1, 8)))
    query_left = scatter_about(streams_of[6], (LAYERS * D, QK), D ** -0.5, 0.0625, ((0, 64),))
    query_right = scatter_about(streams_of[7], (LAYERS * D, QK), D ** -0.5, 0.0625, ((0, 64),))
    return dict(cotangent=cotangent, lengths=lengths, example_ids=example_ids, layer_inputs=layer_inputs, preacts=preacts, weights=weights, query_left=query_left, query_right=query_right)


def silu_slope(preact):
    sigmoid_value = jax.nn.sigmoid(preact)
    return sigmoid_value * (1.0 + preact * (1.0 - sigmoid_value))


def reference(cotangent, lengths, example_ids, layer_inputs, preacts, weights, query_left, query_right):
    seq_slots = jnp.arange(SEQS, dtype=jnp.int32)
    member = (example_ids[:, None] == seq_slots[None, :]).astype(jnp.float32)
    token_len = jnp.dot(member, lengths.astype(jnp.float32), precision=lax.Precision.HIGHEST)
    token_scale = jnp.where(example_ids >= 0, 1.0 / jnp.maximum(token_len, 1.0), 0.0)
    grad_out = (cotangent.astype(jnp.float32) * token_scale[:, None]).astype(jnp.bfloat16)
    scores = jnp.zeros((SEQS, QUERIES), jnp.float32)
    layer_grads = []
    for layer_index in reversed(range(LAYERS)):
        first_col = layer_index * D
        preact = preacts[:, first_col:first_col + D].astype(jnp.float32)
        gate_grad = (silu_slope(preact) * grad_out.astype(jnp.float32)).astype(jnp.bfloat16)
        layer_weight = weights[first_col:first_col + D, :]
        backward = lax.dot_general(gate_grad, layer_weight, (((1,), (1,)), ((), ())), preferred_element_type=jnp.float32)
        in_grad = (grad_out.astype(jnp.float32) + backward).astype(jnp.bfloat16)
        left_part = jnp.dot(layer_inputs[:, first_col:first_col + D], query_left[first_col:first_col + D], preferred_element_type=jnp.float32)
        right_part = jnp.dot(gate_grad, query_right[first_col:first_col + D], preferred_element_type=jnp.float32)
        per_token = jnp.sum((left_part * right_part).reshape(TOKENS, QUERIES, RANK), axis=2)
        scores = scores + jnp.dot(member.T, per_token, precision=lax.Precision.HIGHEST)
        layer_grads.insert(0, in_grad)
        grad_out = in_grad
    return jnp.concatenate(layer_grads, axis=1), scores
```

```python
import jax
import jax.numpy as jnp
from jax import lax
from jax.experimental import pallas as pl
from jax.experimental.pallas import tpu as pltpu
from jax.sharding import PartitionSpec as P

LAYERS = 4
QUERIES = 16
RANK = 16
CHIPS = 8
MICRO = 4
MESH = pl.DeviceIdType.MESH


def silu_slope(preact):
    sigmoid_value = jax.nn.sigmoid(preact)
    return sigmoid_value * (1.0 + preact * (1.0 - sigmoid_value))


def from_behind(value, axis, steps):
    count = lax.axis_size(axis)
    first, last = (max(0, -steps), min(count, count - steps))
    return lax.ppermute(value, axis, [(source, source + steps) for source in range(first, last)])


def row_scale(lens_ref, rows):
    row = lax.broadcasted_iota(jnp.int32, (rows, 1), 0)
    first, second = lens_ref[0], lens_ref[1]
    count = jnp.where(row < first, first, second).astype(jnp.float32)
    return jnp.where(row < first + second, 1.0 / jnp.maximum(count, 1.0), 0.0)


def backward_kernel(
    lens_ref, cot_ref, pre_ref, w_ref, out_ref,
    cot_v, pre_v, w_v, top_v, pre_t, og, gate_v, gates, part_v, parts, ig, nat,
    load_sem, pre_sem, og_sem, gate_sem, part_sem, nat_sem, send_sem,
):
    position, z = lax.axis_index("section"), lax.axis_index("dp")
    s, c, k = position // 16, (position % 16) // 2, position % 2
    rows, cols = pre_v.shape
    tb = rows // MICRO
    diagonal = c == z

    def device(s_, c_, k_, z_):
        return {"section": s_ * 16 + c_ * 2 + k_, "dp": z_}

    def remote(src, dst, phase, sem, where):
        return pltpu.make_async_remote_copy(
            src_ref=src, dst_ref=dst, send_sem=send_sem.at[phase], recv_sem=sem,
            device_id=where, device_id_type=MESH,
        )

    def arrived(ref, sem):
        pltpu.make_async_copy(ref, ref, sem).wait()

    first_col = pl.multiple_of((c * 2 + k) * cols, cols)
    load_cot = pltpu.make_async_copy(cot_ref.at[:, pl.ds(first_col, cols)], cot_v, load_sem.at[0])
    load_pre = pltpu.make_async_copy(pre_ref, pre_v, load_sem.at[1])
    load_w = pltpu.make_async_copy(w_ref, w_v, load_sem.at[2])
    load_cot.start()
    load_pre.start()
    load_w.start()

    barrier = pltpu.get_barrier_semaphore()

    def greet(where):
        pl.semaphore_signal(barrier, inc=1, device_id=where, device_id_type=MESH)

    def greet_layer(i, carry):
        greet(device(s, (c + i // 2) % CHIPS, (k + i % 2) % 2, z))
        return carry

    lax.fori_loop(1, 2 * CHIPS, greet_layer, 0)

    def greet_column(i, carry):
        @pl.when(jnp.logical_not(diagonal & (i == z)))
        def _():
            greet(device(s, z, k, i))
        return carry

    lax.fori_loop(0, CHIPS, greet_column, 0)

    @pl.when(s < LAYERS - 1)
    def _():
        greet(device(s + 1, c, k, z))

    load_cot.wait()
    load_pre.wait()
    top_v[...] = (cot_v[...].astype(jnp.float32) * row_scale(lens_ref, rows)).astype(jnp.bfloat16)

    expected = 3 * CHIPS - 1 - jnp.where(diagonal, 1, 0) + jnp.where(s > 0, 1, 0)
    pl.semaphore_wait(barrier, expected)

    turned = device(s, z, k, c)

    def turn(src, dst, phase, sem):
        @pl.when(diagonal)
        def _():
            pltpu.make_async_copy(src, dst, sem).start()

        @pl.when(jnp.logical_not(diagonal))
        def _():
            remote(src, dst, phase, sem, turned).start()

    for m in range(MICRO):
        block = pl.ds(m * tb, tb)

        @pl.when(s == LAYERS - 1)
        def _():
            turn(top_v.at[block], og.at[m], 0, og_sem.at[m])

        turn(pre_v.at[block], pre_t.at[m], 1, pre_sem.at[m])

    load_w.wait()

    def spread(m):
        arrived(pre_t.at[m], pre_sem.at[m])
        arrived(og.at[m], og_sem.at[m])
        slope = silu_slope(pre_t[m].astype(jnp.float32))
        gate_v[m] = (slope * og[m].astype(jnp.float32)).astype(jnp.bfloat16)
        slot = gates.at[m, k, c]
        pltpu.make_async_copy(gate_v.at[m], slot, gate_sem.at[m]).start()

        def send(i, carry):
            where = device(s, (c + i // 2) % CHIPS, (k + i % 2) % 2, z)
            remote(gate_v.at[m], slot, 2, gate_sem.at[m], where).start()
            return carry

        lax.fori_loop(1, 2 * CHIPS, send, 0)

    def project(m):
        arrived(gates.at[m], gate_sem.at[m])
        total = None
        for half in range(2):
            gate = gates[m, half].reshape(CHIPS * tb, cols)
            term = lax.dot_general(
                gate, w_v[:, half * cols : (half + 1) * cols],
                (((1,), (1,)), ((), ())), preferred_element_type=jnp.float32,
            )
            total = term if total is None else total + term
        part_v[m] = total.astype(jnp.bfloat16).reshape(CHIPS, tb, w_v.shape[0])

        def send(t, carry):
            here = diagonal & (t == c)
            src, dst = part_v.at[m, t], parts.at[m, z]

            @pl.when(here)
            def _():
                pltpu.make_async_copy(src, dst, part_sem.at[m]).start()

            @pl.when(jnp.logical_not(here))
            def _():
                remote(src, dst, 3, part_sem.at[m], device(s, t, k, c)).start()
            return carry

        lax.fori_loop(0, CHIPS, send, 0)

    def collect(m):
        arrived(parts.at[m], part_sem.at[m])
        total = og[m].astype(jnp.float32)
        back = parts[m, 0].astype(jnp.float32)
        for i in range(1, CHIPS):
            back = back + parts[m, i].astype(jnp.float32)
        ig[m] = (total + back).astype(jnp.bfloat16)

        @pl.when(s > 0)
        def _():
            remote(ig.at[m], og.at[m], 4, og_sem.at[m], device(s - 1, c, k, z)).start()

        turn(ig.at[m], nat.at[m], 5, nat_sem.at[m])

    for step, m in ((0, 0), (0, 1), (1, 0), (0, 2), (1, 1), (0, 3), (1, 2), (1, 3), (2, 0), (2, 1), (2, 2), (2, 3)):
        (spread, project, collect)[step](m)

    for m in range(MICRO):
        arrived(nat.at[m], nat_sem.at[m])
        out_ref[m * tb : (m + 1) * tb] = nat[m]

    @pl.when(jnp.logical_not(diagonal))
    def _():
        @pl.when(s == LAYERS - 1)
        def _():
            arrived(og, send_sem.at[0])

        arrived(pre_t, send_sem.at[1])
        arrived(nat, send_sem.at[5])

    for m in range(MICRO):
        arrived(gates.at[m, 0], send_sem.at[2])
        arrived(gates.at[m, 1, : CHIPS - 1], send_sem.at[2])
        arrived(parts.at[m, : CHIPS - 1], send_sem.at[3])

        @pl.when(jnp.logical_not(diagonal))
        def _():
            arrived(parts.at[m, 0], send_sem.at[3])

    @pl.when(s > 0)
    def _():
        arrived(ig, send_sem.at[4])


def run_backward(lengths, cotangent, preacts, weights):
    rows, cols = preacts.shape
    width = weights.shape[0]
    tb = rows // MICRO
    bf16 = jnp.bfloat16
    anywhere = pl.BlockSpec(memory_space=pl.ANY)
    return pl.pallas_call(
        backward_kernel,
        out_shape=jax.ShapeDtypeStruct((rows, cols), bf16),
        in_specs=[pl.BlockSpec(memory_space=pltpu.SMEM), anywhere, anywhere, anywhere],
        out_specs=pl.BlockSpec(memory_space=pltpu.VMEM),
        scratch_shapes=[
            pltpu.VMEM((rows, cols), bf16),
            pltpu.VMEM((rows, cols), bf16),
            pltpu.VMEM(weights.shape, bf16),
            pltpu.VMEM((rows, cols), bf16),
            pltpu.VMEM((MICRO, tb, cols), bf16),
            pltpu.VMEM((MICRO, tb, cols), bf16),
            pltpu.VMEM((MICRO, tb, cols), bf16),
            pltpu.VMEM((MICRO, 2, CHIPS, tb, cols), bf16),
            pltpu.VMEM((MICRO, CHIPS, tb, width), bf16),
            pltpu.VMEM((MICRO, CHIPS, tb, width), bf16),
            pltpu.VMEM((MICRO, tb, cols), bf16),
            pltpu.VMEM((MICRO, tb, cols), bf16),
            pltpu.SemaphoreType.DMA((3,)),
            pltpu.SemaphoreType.DMA((MICRO,)),
            pltpu.SemaphoreType.DMA((MICRO,)),
            pltpu.SemaphoreType.DMA((MICRO,)),
            pltpu.SemaphoreType.DMA((MICRO,)),
            pltpu.SemaphoreType.DMA((MICRO,)),
            pltpu.SemaphoreType.DMA((6,)),
        ],
        compiler_params=pltpu.CompilerParams(collective_id=0, has_side_effects=True),
    )(lengths, cotangent, preacts, weights)


def per_device(
    cotangent, lengths, example_ids, layer_inputs, preacts, weights, query_left, query_right
):
    per_section = lax.axis_size("section") // LAYERS
    position = lax.axis_index("section")
    section_index, column_block = position // per_section, position % per_section
    group_index = lax.axis_index("dp")
    seq_count, block_cols = lengths.shape[0], layer_inputs.shape[1]
    in_grad = run_backward(lengths, cotangent, preacts, weights)

    seq_slots = group_index * seq_count + jnp.arange(seq_count, dtype=jnp.int32)
    member = (example_ids[:, None] == seq_slots[None, :]).astype(jnp.float32)
    token_len = jnp.dot(member, lengths.astype(jnp.float32), precision=lax.Precision.HIGHEST)
    token_scale = jnp.where(example_ids >= 0, 1.0 / jnp.maximum(token_len, 1.0), 0.0)
    top_columns = lax.dynamic_slice_in_dim(cotangent, column_block * block_cols, block_cols, 1)
    top_grad = (top_columns.astype(jnp.float32) * token_scale[:, None]).astype(jnp.bfloat16)
    arrived = from_behind(in_grad, "section", -per_section)
    out_grad = jnp.where(section_index == LAYERS - 1, top_grad, arrived)
    slope = silu_slope(preacts.astype(jnp.float32))
    gate_grad = (slope * out_grad.astype(jnp.float32)).astype(jnp.bfloat16)
    left = jnp.dot(layer_inputs, query_left, preferred_element_type=jnp.float32)
    right = jnp.dot(gate_grad, query_right, preferred_element_type=jnp.float32)
    groups = [[g * per_section + i for i in range(per_section)] for g in range(LAYERS)]
    both = lax.psum(jnp.concatenate([left, right], axis=1), "section", axis_index_groups=groups)
    product = both[:, : QUERIES * RANK] * both[:, QUERIES * RANK :]
    per_token = jnp.sum(product.reshape(-1, QUERIES, RANK), axis=2)
    scores = jnp.dot(member.T, per_token, precision=lax.Precision.HIGHEST)
    scores = lax.psum(scores, "section") * (1.0 / per_section)
    return (in_grad, scores)


def solution(mesh):
    placed = (
        P("dp", None),
        P("dp"),
        P("dp"),
        P("dp", "section"),
        P("dp", "section"),
        P("section", "dp"),
        P("section", None),
        P("section", None),
    )
    return jax.shard_map(
        per_device,
        mesh=mesh,
        in_specs=placed,
        out_specs=(P("dp", "section"), P("dp", None)),
        check_vma=False,
    )
```

```python
import jax
import jax.numpy as jnp
from jax import lax
from jax.experimental import pallas as pl
from jax.experimental.pallas import tpu as pltpu
from jax.sharding import PartitionSpec as P

LAYERS = 4
QUERIES = 16
RANK = 16
CHIPS = 8
MICRO = 4
MESH = pl.DeviceIdType.MESH
ORDER = (
    ("s", 0), ("s", 1), ("p", 0), ("s", 2), ("p", 1), ("s", 3), ("p", 2), ("c", 0),
    ("p", 3), ("r", 0), ("c", 1), ("c", 2), ("c", 3), ("r", 1), ("r", 2), ("r", 3),
)


def silu_slope(preact):
    sigmoid_value = jax.nn.sigmoid(preact)
    return sigmoid_value * (1.0 + preact * (1.0 - sigmoid_value))


def influence_kernel(
    lens_ref, cot_ref, in_ref, pre_ref, w_ref, left_ref, right_ref, grads_ref, scores_ref,
    cot_v, in_v, pre_v, w_v, left_v, right_v, low_pre, og, top_gate, next_gate, gates,
    part_v, parts, ig, sides, side_in, per_row, row_in, layer_sum, layer_in,
    load_sem, pre_sem, og_sem, turn_sem, gate_sem, core_sem, part_sem, score_sem, send_sem,
):
    position, z = lax.axis_index("section"), lax.axis_index("dp")
    s, c, k = position // 16, (position % 16) // 2, position % 2
    rows, cols = pre_v.shape
    tb = rows // MICRO
    half = QUERIES * RANK // 2
    top = s == LAYERS - 1
    f32, bf16 = jnp.float32, jnp.bfloat16
    me = c * 2 + k

    def device(s_, c_, k_, z_):
        return {"section": s_ * 16 + c_ * 2 + k_, "dp": z_}

    def in_layer(i):
        return (c + i // 2) % CHIPS, (k + i % 2) % 2

    def remote(src, dst, phase, sem, where):
        pltpu.make_async_remote_copy(
            src_ref=src, dst_ref=dst, send_sem=send_sem.at[phase], recv_sem=sem,
            device_id=where, device_id_type=MESH,
        ).start()

    def arrived(ref, sem):
        pltpu.make_async_copy(ref, ref, sem).wait()

    def each(first, last, body):
        def step(i, carry):
            body(i)
            return carry

        lax.fori_loop(first, last, step, 0)

    first_col = pl.multiple_of(me * cols, cols)
    loads = [
        pltpu.make_async_copy(cot_ref.at[:, pl.ds(first_col, cols)], cot_v, load_sem.at[0]),
        pltpu.make_async_copy(pre_ref, pre_v, load_sem.at[1]),
        pltpu.make_async_copy(w_ref.at[:, pl.ds(0, cols)], w_v.at[0], load_sem.at[2]),
        pltpu.make_async_copy(w_ref.at[:, pl.ds(cols, cols)], w_v.at[1], load_sem.at[3]),
        pltpu.make_async_copy(in_ref, in_v, load_sem.at[4]),
        pltpu.make_async_copy(left_ref, left_v, load_sem.at[5]),
        pltpu.make_async_copy(right_ref, right_v, load_sem.at[6]),
    ]
    for load in loads:
        load.start()

    barrier = pltpu.get_barrier_semaphore()

    def greet(where):
        pl.semaphore_signal(barrier, inc=1, device_id=where, device_id_type=MESH)

    greet(device(jnp.minimum(s + 1, LAYERS - 1), z, k, (c + 6 * z + 7) % CHIPS))
    each(1, LAYERS, lambda i: greet(device((s + i) % LAYERS, c, k, z)))
    each(1, CHIPS, lambda i: greet(device(s, c, k, (z + i) % CHIPS)))
    each(1, 2 * CHIPS, lambda i: greet(device(s, *in_layer(i), z)))

    first, second = lens_ref[0], lens_ref[1]
    row = lax.broadcasted_iota(jnp.int32, (rows, 1), 0)
    count = jnp.where(row < first, first, second).astype(f32)
    scale = jnp.where(row < first + second, 1.0 / jnp.maximum(count, 1.0), 0.0)
    loads[0].wait()
    loads[1].wait()

    @pl.when(top)
    def _():
        for m in range(MICRO):
            block = pl.ds(m * tb, tb)
            top_rows = (cot_v[block].astype(f32) * scale[m * tb : (m + 1) * tb]).astype(bf16)
            og[m] = top_rows
            slope = silu_slope(pre_v[block].astype(f32))
            top_gate[m] = (slope * top_rows.astype(f32)).astype(bf16)

    expected = 2 * CHIPS - 1 + CHIPS - 1 + LAYERS - 1
    expected = expected + jnp.where(s > 0, 1, 0) + jnp.where(top, 1, 0)
    pl.semaphore_wait(barrier, expected)

    turn = (2 * c + z + 1) % CHIPS

    @pl.when(top)
    def _():
        for m in range(MICRO):
            remote(top_gate.at[m], gates.at[m, k, turn], 0, turn_sem.at[m], device(s, turn, k, c))

    @pl.when(s < LAYERS - 1)
    def _():
        remote(pre_v, low_pre, 3, pre_sem.at[0], device(s + 1, c, k, z))

    for load in loads[2:]:
        load.wait()
    left = jnp.dot(in_v[...], left_v[...], preferred_element_type=f32)
    for h in range(2):
        sides[h, :, :half] = left[:, h * half : (h + 1) * half]

    @pl.when(s > 0)
    def _():
        arrived(low_pre, pre_sem.at[0])

    def spread(m):
        mine = gates.at[m, k, c]
        arrived(mine, turn_sem.at[m])
        each(1, CHIPS, lambda i: remote(
            mine, mine, 4, gate_sem.at[m], device(s, (c + i) % CHIPS, k, z)))

    def project(m):
        arrived(gates.at[m, 0, : CHIPS - 1], gate_sem.at[m])
        remote(gates.at[m, k], gates.at[m, k], 5, core_sem.at[m], device(s, c, 1 - k, z))

        def product(h):
            return lax.dot_general(
                gates[m, h].reshape(CHIPS * tb, cols), w_v[h],
                (((1,), (1,)), ((), ())), preferred_element_type=f32,
            )

        total = product(k)
        arrived(gates.at[m, 0], core_sem.at[m])
        total = total + product(1 - k)
        part_v[m] = total.astype(bf16).reshape(CHIPS, tb, cols)

        def send(i):
            t = (z + i) % CHIPS
            remote(part_v.at[m, (t + 2 * z + 1) % CHIPS], parts.at[m, z], 6, part_sem.at[m],
                   device(s, c, k, t))

        each(1, CHIPS, send)
        parts[m, z] = part_v[m, (3 * z + 1) % CHIPS]

        @pl.when(s < LAYERS - 1)
        def _():
            arrived(og.at[m], og_sem.at[m])

    def collect(m):
        arrived(parts.at[m, : CHIPS - 1], part_sem.at[m])
        back = parts[m, 0].astype(f32)
        for i in range(1, CHIPS):
            back = back + parts[m, i].astype(f32)
        in_grad = (og[m].astype(f32) + back).astype(bf16)
        block = pl.ds(m * tb, tb)
        grads_ref[block] = in_grad

        @pl.when(s > 0)
        def _():
            slope = silu_slope(low_pre[block].astype(f32))
            next_gate[m] = (slope * in_grad.astype(f32)).astype(bf16)
            ig[m] = in_grad
            remote(next_gate.at[m], gates.at[m, k, turn], 1, turn_sem.at[m],
                   device(s - 1, turn, k, c))
            remote(ig.at[m], og.at[m], 2, og_sem.at[m], device(s - 1, c, k, z))

    def score(step):
        if step == 0:
            slope = silu_slope(pre_v[...].astype(f32))
            gate = (slope * og[...].reshape(rows, cols).astype(f32)).astype(bf16)
            right = jnp.dot(gate, right_v[...], preferred_element_type=f32)
            for h in range(2):
                sides[h, :, half:] = right[:, h * half : (h + 1) * half]

            def send(i):
                c_, k_ = in_layer(i)
                eight = pl.ds(pl.multiple_of(c_ * 8, 8), 8)
                remote(sides.at[k_, eight], side_in.at[me], 7, score_sem.at[0],
                       device(s, c_, k_, z))

            each(1, 2 * CHIPS, send)
            side_in[me] = sides[k, pl.ds(pl.multiple_of(c * 8, 8), 8)]
        elif step == 1:
            arrived(side_in.at[: 2 * CHIPS - 1], score_sem.at[0])
            both = side_in[0]
            for i in range(1, 2 * CHIPS):
                both = both + side_in[i]
            product = both[:, :half] * both[:, half:]
            eight = lax.broadcasted_iota(jnp.int32, (8, half), 0)
            token = eight + c * 8
            one = jnp.sum(jnp.where(token < first, product, 0.0), axis=0, keepdims=True)
            later = (token >= first) & (token < first + second)
            two = jnp.sum(jnp.where(later, product, 0.0), axis=0, keepdims=True)
            per_row[...] = jnp.where(eight == 0, one, jnp.where(eight == 1, two, 0.0))
            each(1, 2 * CHIPS, lambda i: remote(
                per_row, row_in.at[me], 8, score_sem.at[1], device(s, *in_layer(i), z)))
            row_in[me] = per_row[...]
        elif step == 2:
            arrived(row_in.at[: 2 * CHIPS - 1], score_sem.at[1])
            for h in range(2):
                total = row_in[h]
                for i in range(1, CHIPS):
                    total = total + row_in[2 * i + h]
                layer_sum[:, h * half : (h + 1) * half] = total
            each(1, LAYERS, lambda i: remote(
                layer_sum, layer_in.at[s], 9, score_sem.at[2], device((s + i) % LAYERS, c, k, z)))
            layer_in[s] = layer_sum[...]
        else:
            arrived(layer_in.at[: LAYERS - 1], score_sem.at[2])
            total = layer_in[0]
            for i in range(1, LAYERS):
                total = total + layer_in[i]
            lane = lax.broadcasted_iota(jnp.int32, (2 * half, QUERIES), 0) // RANK
            query = lax.broadcasted_iota(jnp.int32, (2 * half, QUERIES), 1)
            pick = jnp.where(lane == query, 1.0, 0.0).astype(f32)
            summed = jnp.dot(total, pick, precision=lax.Precision.HIGHEST,
                             preferred_element_type=f32)
            scores_ref[...] = summed[: scores_ref.shape[0]]

    events = dict(s=spread, p=project, c=collect, r=score)
    for event, m in ORDER:
        events[event](m)

    @pl.when(top)
    def _():
        arrived(top_gate, send_sem.at[0])

    @pl.when(s > 0)
    def _():
        arrived(next_gate, send_sem.at[1])
        arrived(ig, send_sem.at[2])

    @pl.when(s < LAYERS - 1)
    def _():
        arrived(pre_v, send_sem.at[3])

    arrived(gates.at[:, 0, : CHIPS - 1], send_sem.at[4])
    arrived(gates.at[:, 0], send_sem.at[5])
    arrived(parts.at[:, : CHIPS - 1], send_sem.at[6])
    arrived(side_in.at[: 2 * CHIPS - 1], send_sem.at[7])
    arrived(row_in.at[: 2 * CHIPS - 1], send_sem.at[8])
    arrived(layer_in.at[: LAYERS - 1], send_sem.at[9])


def per_device(
    cotangent, lengths, example_ids, layer_inputs, preacts, weights, query_left, query_right
):
    rows, cols = preacts.shape
    tb = rows // MICRO
    width = QUERIES * RANK
    bf16, f32 = jnp.bfloat16, jnp.float32
    anywhere = pl.BlockSpec(memory_space=pl.ANY)
    in_vmem = pl.BlockSpec(memory_space=pltpu.VMEM)
    chunk = pltpu.VMEM((MICRO, tb, cols), bf16)
    block = pltpu.VMEM((rows, cols), bf16)
    sems = pltpu.SemaphoreType.DMA
    return pl.pallas_call(
        influence_kernel,
        out_shape=(
            jax.ShapeDtypeStruct((rows, cols), bf16),
            jax.ShapeDtypeStruct((lengths.shape[0], QUERIES), f32),
        ),
        in_specs=[pl.BlockSpec(memory_space=pltpu.SMEM)] + [anywhere] * 6,
        out_specs=(in_vmem, in_vmem),
        scratch_shapes=[
            block, block, block,
            pltpu.VMEM((2, cols, cols), bf16),
            pltpu.VMEM(query_left.shape, bf16),
            pltpu.VMEM(query_right.shape, bf16),
            block, chunk, chunk, chunk,
            pltpu.VMEM((MICRO, 2, CHIPS, tb, cols), bf16),
            pltpu.VMEM((MICRO, CHIPS, tb, cols), bf16),
            pltpu.VMEM((MICRO, CHIPS, tb, cols), bf16),
            chunk,
            pltpu.VMEM((2, rows, width), f32),
            pltpu.VMEM((2 * CHIPS, 8, width), f32),
            pltpu.VMEM((8, width // 2), f32),
            pltpu.VMEM((2 * CHIPS, 8, width // 2), f32),
            pltpu.VMEM((8, width), f32),
            pltpu.VMEM((LAYERS, 8, width), f32),
            sems((7,)), sems((1,)), sems((MICRO,)), sems((MICRO,)), sems((MICRO,)),
            sems((MICRO,)), sems((MICRO,)), sems((3,)), sems((10,)),
        ],
        compiler_params=pltpu.CompilerParams(collective_id=0, has_side_effects=True),
    )(lengths, cotangent, layer_inputs, preacts, weights, query_left, query_right)


def solution(mesh):
    placed = (
        P("dp", None),
        P("dp"),
        P("dp"),
        P("dp", "section"),
        P("dp", "section"),
        P("section", "dp"),
        P("section", None),
        P("section", None),
    )
    return jax.shard_map(
        per_device,
        mesh=mesh,
        in_specs=placed,
        out_specs=(P("dp", "section"), P("dp", None)),
        check_vma=False,
    )
```

```python
import jax
import jax.numpy as jnp
from jax import lax
from jax.experimental import pallas as pl
from jax.experimental.pallas import tpu as pltpu
from jax.sharding import PartitionSpec as P

LAYERS = 4
QUERIES = 16
RANK = 16
CHIPS = 8
MICRO = 4
MESH = pl.DeviceIdType.MESH
ORDER = (
    ("s", 0), ("s", 1), ("p", 0), ("s", 2), ("p", 1), ("e", 0), ("s", 3), ("p", 2), ("e", 1), ("c", 0),
    ("p", 3), ("c", 1), ("e", 2), ("c", 2), ("c", 3), ("l", 0), ("l", 1), ("l", 2), ("r", 3),
)
ROUTE = ((0, 2), (0, 1), (0, 0), (1, 1), (1, 0), (1, 3), (1, 2), (0, 3))


def silu_slope(preact):
    sigmoid_value = jax.nn.sigmoid(preact)
    return sigmoid_value * (1.0 + preact * (1.0 - sigmoid_value))


def looked_up(table, index):
    value = jnp.int32(table[0])
    for i in range(1, len(table)):
        value = jnp.where(index == i, table[i], value)
    return value


def chip_of(plane, source):
    away = (source + CHIPS - plane) % CHIPS
    row, step = (looked_up([pair[i] for pair in ROUTE], away) for i in range(2))
    return row * 4 + (plane + step) % 4


def source_of(plane, chip):
    away = [0] * CHIPS
    for i, (row, step) in enumerate(ROUTE):
        away[row * 4 + step] = i
    return (plane + looked_up(away, chip // 4 * 4 + (chip + 4 - plane % 4) % 4)) % CHIPS


def influence_kernel(
    lens_ref, cot_ref, in_ref, pre_ref, w_ref, left_ref, right_ref, grads_ref, scores_ref,
    cot_v, in_v, pre_v, w_v, left_v, right_v, low_pre, low_slope, own_slope, og, top_gate, next_gate, gates,
    part_v, parts, ig, sides, side_in, per_row, row_in, layer_sum, layer_in,
    load_sem, pre_sem, og_sem, turn_sem, gate_sem, core_sem, part_sem, score_sem, send_sem,
):
    position, z = lax.axis_index("section"), lax.axis_index("dp")
    s, c, k = position // 16, (position % 16) // 2, position % 2
    rows, cols = pre_v.shape
    tb = rows // MICRO
    half = QUERIES * RANK // 2
    top = s == LAYERS - 1
    f32, bf16 = jnp.float32, jnp.bfloat16
    me = c * 2 + k

    def device(s_, c_, k_, z_):
        return {"section": s_ * 16 + c_ * 2 + k_, "dp": z_}

    def in_layer(i):
        return (c + i // 2) % CHIPS, (k + i % 2) % 2

    def remote(src, dst, phase, sem, where):
        pltpu.make_async_remote_copy(
            src_ref=src, dst_ref=dst, send_sem=send_sem.at[phase], recv_sem=sem,
            device_id=where, device_id_type=MESH,
        ).start()

    def arrived(ref, sem):
        pltpu.make_async_copy(ref, ref, sem).wait()

    def each(first, last, body):
        def step(i, carry):
            body(i)
            return carry

        lax.fori_loop(first, last, step, 0)

    first_col = pl.multiple_of(me * cols, cols)
    loads = [
        pltpu.make_async_copy(cot_ref.at[:, pl.ds(first_col, cols)], cot_v, load_sem.at[0]),
        pltpu.make_async_copy(pre_ref, pre_v, load_sem.at[1]),
        pltpu.make_async_copy(w_ref.at[:, pl.ds(0, cols)], w_v.at[0], load_sem.at[2]),
        pltpu.make_async_copy(w_ref.at[:, pl.ds(cols, cols)], w_v.at[1], load_sem.at[3]),
        pltpu.make_async_copy(in_ref, in_v, load_sem.at[4]),
        pltpu.make_async_copy(left_ref, left_v, load_sem.at[5]),
        pltpu.make_async_copy(right_ref, right_v, load_sem.at[6]),
    ]
    for load in loads:
        load.start()

    barrier = pltpu.get_barrier_semaphore()

    def greet(where):
        pl.semaphore_signal(barrier, inc=1, device_id=where, device_id_type=MESH)

    greet(device(jnp.minimum(s + 1, LAYERS - 1), z, k, source_of(z, c)))
    each(1, LAYERS, lambda i: greet(device((s + i) % LAYERS, c, k, z)))
    each(1, CHIPS, lambda i: greet(device(s, c, k, (z + i) % CHIPS)))
    each(1, 2 * CHIPS, lambda i: greet(device(s, *in_layer(i), z)))

    first, second = lens_ref[0], lens_ref[1]
    row = lax.broadcasted_iota(jnp.int32, (rows, 1), 0)
    count = jnp.where(row < first, first, second).astype(f32)
    scale = jnp.where(row < first + second, 1.0 / jnp.maximum(count, 1.0), 0.0)
    loads[0].wait()
    loads[1].wait()

    @pl.when(top)
    def _():
        for m in range(MICRO):
            block = pl.ds(m * tb, tb)
            top_rows = (cot_v[block].astype(f32) * scale[m * tb : (m + 1) * tb]).astype(bf16)
            og[m] = top_rows
            slope = silu_slope(pre_v[block].astype(f32))
            top_gate[m] = (slope * top_rows.astype(f32)).astype(bf16)

    expected = 2 * CHIPS - 1 + CHIPS - 1 + LAYERS - 1
    expected = expected + jnp.where(s > 0, 1, 0) + jnp.where(top, 1, 0)
    pl.semaphore_wait(barrier, expected)

    turn = chip_of(c, z)

    @pl.when(top)
    def _():
        for m in range(MICRO):
            remote(top_gate.at[m], gates.at[m, k, turn], 0, turn_sem.at[m], device(s, turn, k, c))

    @pl.when(s < LAYERS - 1)
    def _():
        remote(pre_v, low_pre, 3, pre_sem.at[0], device(s + 1, c, k, z))

    for load in loads[2:]:
        load.wait()
    left = jnp.dot(in_v[...], left_v[...], preferred_element_type=f32)
    for h in range(2):
        sides[h, :, :half] = left[:, h * half : (h + 1) * half]
    own_slope[...] = silu_slope(pre_v[...].astype(f32))

    @pl.when(s > 0)
    def _():
        arrived(low_pre, pre_sem.at[0])
        low_slope[...] = silu_slope(low_pre[...].astype(f32))

    def spread(m):
        mine = gates.at[m, k, c]
        arrived(mine, turn_sem.at[m])
        each(1, CHIPS, lambda i: remote(
            mine, mine, 4, gate_sem.at[m], device(s, (c + i) % CHIPS, k, z)))

    def project(m):
        arrived(gates.at[m, 0, : CHIPS - 1], gate_sem.at[m])
        remote(gates.at[m, k], gates.at[m, k], 5, core_sem.at[m], device(s, c, 1 - k, z))

        def product(h):
            return lax.dot_general(
                gates[m, h].reshape(CHIPS * tb, cols), w_v[h],
                (((1,), (1,)), ((), ())), preferred_element_type=f32,
            )

        total = product(k)
        arrived(gates.at[m, 0], core_sem.at[m])
        total = total + product(1 - k)
        part_v[m] = total.astype(bf16).reshape(CHIPS, tb, cols)

        def send(i):
            t = (z + i) % CHIPS
            remote(part_v.at[m, chip_of(z, t)], parts.at[m, z], 6, part_sem.at[m],
                   device(s, c, k, t))

        each(1, CHIPS, send)
        parts[m, z] = part_v[m, chip_of(z, z)]

    def wait_residual(m, which):
        @pl.when(which)
        def _():
            arrived(og.at[m], og_sem.at[m])

    def collect(m):
        wait_residual(m, (s > 0) & (s < LAYERS - 1))
        arrived(parts.at[m, : CHIPS - 1], part_sem.at[m])
        back = parts[m, 0].astype(f32)
        for i in range(1, CHIPS):
            back = back + parts[m, i].astype(f32)
        in_grad = (og[m].astype(f32) + back).astype(bf16)
        block = pl.ds(m * tb, tb)
        grads_ref[block] = in_grad

        @pl.when(s > 0)
        def _():
            next_gate[m] = (low_slope[block] * in_grad.astype(f32)).astype(bf16)
            ig[m] = in_grad
            remote(next_gate.at[m], gates.at[m, k, turn], 1, turn_sem.at[m],
                   device(s - 1, turn, k, c))
            remote(ig.at[m], og.at[m], 2, og_sem.at[m], device(s - 1, c, k, z))

    def score(step):
        if step == 0:
            for m in range(MICRO):
                wait_residual(m, s == 0)
            gate = (own_slope[...] * og[...].reshape(rows, cols).astype(f32)).astype(bf16)
            right = jnp.dot(gate, right_v[...], preferred_element_type=f32)
            for h in range(2):
                sides[h, :, half:] = right[:, h * half : (h + 1) * half]

            def send(i):
                c_, k_ = in_layer(i)
                eight = pl.ds(pl.multiple_of(c_ * 8, 8), 8)
                remote(sides.at[k_, eight], side_in.at[me], 7, score_sem.at[0],
                       device(s, c_, k_, z))

            each(1, 2 * CHIPS, send)
            side_in[me] = sides[k, pl.ds(pl.multiple_of(c * 8, 8), 8)]
        elif step == 1:
            arrived(side_in.at[: 2 * CHIPS - 1], score_sem.at[0])
            both = side_in[0]
            for i in range(1, 2 * CHIPS):
                both = both + side_in[i]
            product = both[:, :half] * both[:, half:]
            eight = lax.broadcasted_iota(jnp.int32, (8, half), 0)
            token = eight + c * 8
            one = jnp.sum(jnp.where(token < first, product, 0.0), axis=0, keepdims=True)
            later = (token >= first) & (token < first + second)
            two = jnp.sum(jnp.where(later, product, 0.0), axis=0, keepdims=True)
            per_row[...] = jnp.where(eight == 0, one, jnp.where(eight == 1, two, 0.0))
            each(1, 2 * CHIPS, lambda i: remote(
                per_row, row_in.at[me], 8, score_sem.at[1], device(s, *in_layer(i), z)))
            row_in[me] = per_row[...]
        elif step == 2:
            arrived(row_in.at[: 2 * CHIPS - 1], score_sem.at[1])
            for h in range(2):
                total = row_in[h]
                for i in range(1, CHIPS):
                    total = total + row_in[2 * i + h]
                layer_sum[:, h * half : (h + 1) * half] = total
            each(1, LAYERS, lambda i: remote(
                layer_sum, layer_in.at[s], 9, score_sem.at[2], device((s + i) % LAYERS, c, k, z)))
            layer_in[s] = layer_sum[...]
        else:
            arrived(layer_in.at[: LAYERS - 1], score_sem.at[2])
            total = layer_in[0]
            for i in range(1, LAYERS):
                total = total + layer_in[i]
            lane = lax.broadcasted_iota(jnp.int32, (2 * half, QUERIES), 0) // RANK
            query = lax.broadcasted_iota(jnp.int32, (2 * half, QUERIES), 1)
            pick = jnp.where(lane == query, 1.0, 0.0).astype(f32)
            summed = jnp.dot(total, pick, precision=lax.Precision.HIGHEST,
                             preferred_element_type=f32)
            scores_ref[...] = summed[: scores_ref.shape[0]]

    def early(step):
        @pl.when(s == 0)
        def _():
            score(step)

    def late(step):
        @pl.when(s > 0)
        def _():
            score(step)

    events = dict(s=spread, p=project, c=collect, r=score, e=early, l=late)
    for event, m in ORDER:
        events[event](m)

    @pl.when(top)
    def _():
        arrived(top_gate, send_sem.at[0])

    @pl.when(s > 0)
    def _():
        arrived(next_gate, send_sem.at[1])
        arrived(ig, send_sem.at[2])

    @pl.when(s < LAYERS - 1)
    def _():
        arrived(pre_v, send_sem.at[3])

    arrived(gates.at[:, 0, : CHIPS - 1], send_sem.at[4])
    arrived(gates.at[:, 0], send_sem.at[5])
    arrived(parts.at[:, : CHIPS - 1], send_sem.at[6])
    arrived(side_in.at[: 2 * CHIPS - 1], send_sem.at[7])
    arrived(row_in.at[: 2 * CHIPS - 1], send_sem.at[8])
    arrived(layer_in.at[: LAYERS - 1], send_sem.at[9])


def per_device(
    cotangent, lengths, example_ids, layer_inputs, preacts, weights, query_left, query_right
):
    rows, cols = preacts.shape
    tb = rows // MICRO
    width = QUERIES * RANK
    bf16, f32 = jnp.bfloat16, jnp.float32
    anywhere = pl.BlockSpec(memory_space=pl.ANY)
    in_vmem = pl.BlockSpec(memory_space=pltpu.VMEM)
    chunk = pltpu.VMEM((MICRO, tb, cols), bf16)
    block = pltpu.VMEM((rows, cols), bf16)
    sems = pltpu.SemaphoreType.DMA
    return pl.pallas_call(
        influence_kernel,
        out_shape=(
            jax.ShapeDtypeStruct((rows, cols), bf16),
            jax.ShapeDtypeStruct((lengths.shape[0], QUERIES), f32),
        ),
        in_specs=[pl.BlockSpec(memory_space=pltpu.SMEM)] + [anywhere] * 6,
        out_specs=(in_vmem, in_vmem),
        scratch_shapes=[
            block, block, block,
            pltpu.VMEM((2, cols, cols), bf16),
            pltpu.VMEM(query_left.shape, bf16),
            pltpu.VMEM(query_right.shape, bf16),
            block, pltpu.VMEM((rows, cols), f32), pltpu.VMEM((rows, cols), f32), chunk, chunk, chunk,
            pltpu.VMEM((MICRO, 2, CHIPS, tb, cols), bf16),
            pltpu.VMEM((MICRO, CHIPS, tb, cols), bf16),
            pltpu.VMEM((MICRO, CHIPS, tb, cols), bf16),
            chunk,
            pltpu.VMEM((2, rows, width), f32),
            pltpu.VMEM((2 * CHIPS, 8, width), f32),
            pltpu.VMEM((8, width // 2), f32),
            pltpu.VMEM((2 * CHIPS, 8, width // 2), f32),
            pltpu.VMEM((8, width), f32),
            pltpu.VMEM((LAYERS, 8, width), f32),
            sems((7,)), sems((1,)), sems((MICRO,)), sems((MICRO,)), sems((MICRO,)),
            sems((MICRO,)), sems((MICRO,)), sems((3,)), sems((10,)),
        ],
        compiler_params=pltpu.CompilerParams(collective_id=0, has_side_effects=True),
    )(lengths, cotangent, layer_inputs, preacts, weights, query_left, query_right)


def solution(mesh):
    placed = (
        P("dp", None),
        P("dp"),
        P("dp"),
        P("dp", "section"),
        P("dp", "section"),
        P("section", "dp"),
        P("section", None),
        P("section", None),
    )
    return jax.shard_map(
        per_device,
        mesh=mesh,
        in_specs=placed,
        out_specs=(P("dp", "section"), P("dp", None)),
        check_vma=False,
    )
```

```python
import jax
import jax.numpy as jnp
from jax import lax
from jax.experimental import pallas as pl
from jax.experimental.pallas import tpu as pltpu
from jax.sharding import PartitionSpec as P

LAYERS = 4
QUERIES = 16
RANK = 16
CHIPS = 8
MICRO = 8
MESH = pl.DeviceIdType.MESH
ORDER = (
    ("s", 0), ("s", 1), ("s", 2), ("s", 3), ("x", 0), ("s", 4), ("x", 1), ("p", 0), ("s", 5), ("x", 2), ("p", 1), ("s", 6), ("x", 3), ("p", 2), ("e", 0), ("s", 7), ("x", 4), ("p", 3), ("x", 5), ("c", 0), ("p", 4), ("x", 6), ("c", 1), ("p", 5), ("x", 7), ("c", 2), ("p", 6), ("e", 1), ("c", 3), ("p", 7), ("c", 4), ("c", 5), ("e", 2), ("c", 6), ("c", 7), ("l", 0), ("l", 1), ("l", 2), ("r", 3),
)
ROUTE = ((0, 2), (0, 1), (0, 0), (1, 1), (1, 0), (1, 3), (1, 2), (0, 3))


def silu_slope(preact):
    sigmoid_value = jax.nn.sigmoid(preact)
    return sigmoid_value * (1.0 + preact * (1.0 - sigmoid_value))


def looked_up(table, index):
    value = jnp.int32(table[0])
    for i in range(1, len(table)):
        value = jnp.where(index == i, table[i], value)
    return value


def chip_of(plane, source):
    away = (source + CHIPS - plane) % CHIPS
    row, step = (looked_up([pair[i] for pair in ROUTE], away) for i in range(2))
    return row * 4 + (plane + step) % 4


def source_of(plane, chip):
    away = [0] * CHIPS
    for i, (row, step) in enumerate(ROUTE):
        away[row * 4 + step] = i
    return (plane + looked_up(away, chip // 4 * 4 + (chip + 4 - plane % 4) % 4)) % CHIPS


def influence_kernel(
    lens_ref, cot_ref, in_ref, pre_ref, w_ref, left_ref, right_ref, grads_ref, scores_ref,
    cot_v, in_v, pre_v, w_v, left_v, right_v, low_pre, low_slope, own_slope, og, top_gate, next_gate, gates,
    half_product, part_v, parts, ig, sides, side_in, per_row, row_in, layer_sum, layer_in,
    load_sem, pre_sem, og_sem, turn_sem, gate_sem, core_sem, part_sem, score_sem, send_sem,
):
    position, z = lax.axis_index("section"), lax.axis_index("dp")
    s, c, k = position // 16, (position % 16) // 2, position % 2
    rows, cols = pre_v.shape
    tb = rows // MICRO
    half = QUERIES * RANK // 2
    top = s == LAYERS - 1
    f32, bf16 = jnp.float32, jnp.bfloat16
    me = c * 2 + k

    def device(s_, c_, k_, z_):
        return {"section": s_ * 16 + c_ * 2 + k_, "dp": z_}

    def in_layer(i):
        return (c + i // 2) % CHIPS, (k + i % 2) % 2

    def remote(src, dst, phase, sem, where):
        pltpu.make_async_remote_copy(
            src_ref=src, dst_ref=dst, send_sem=send_sem.at[phase], recv_sem=sem,
            device_id=where, device_id_type=MESH,
        ).start()

    def arrived(ref, sem):
        pltpu.make_async_copy(ref, ref, sem).wait()

    def each(first, last, body):
        def step(i, carry):
            body(i)
            return carry

        lax.fori_loop(first, last, step, 0)

    first_col = pl.multiple_of(me * cols, cols)
    loads = [
        pltpu.make_async_copy(cot_ref.at[:, pl.ds(first_col, cols)], cot_v, load_sem.at[0]),
        pltpu.make_async_copy(pre_ref, pre_v, load_sem.at[1]),
        pltpu.make_async_copy(w_ref.at[:, pl.ds(0, cols)], w_v.at[0], load_sem.at[2]),
        pltpu.make_async_copy(w_ref.at[:, pl.ds(cols, cols)], w_v.at[1], load_sem.at[3]),
        pltpu.make_async_copy(in_ref, in_v, load_sem.at[4]),
        pltpu.make_async_copy(left_ref, left_v, load_sem.at[5]),
        pltpu.make_async_copy(right_ref, right_v, load_sem.at[6]),
    ]
    for load in loads:
        load.start()

    barrier = pltpu.get_barrier_semaphore()

    def greet(where):
        pl.semaphore_signal(barrier, inc=1, device_id=where, device_id_type=MESH)

    greet(device(jnp.minimum(s + 1, LAYERS - 1), z, k, source_of(z, c)))
    each(1, LAYERS, lambda i: greet(device((s + i) % LAYERS, c, k, z)))
    each(1, CHIPS, lambda i: greet(device(s, c, k, (z + i) % CHIPS)))
    each(1, 2 * CHIPS, lambda i: greet(device(s, *in_layer(i), z)))

    first, second = lens_ref[0], lens_ref[1]
    row = lax.broadcasted_iota(jnp.int32, (rows, 1), 0)
    count = jnp.where(row < first, first, second).astype(f32)
    scale = jnp.where(row < first + second, 1.0 / jnp.maximum(count, 1.0), 0.0)
    loads[0].wait()
    loads[1].wait()

    @pl.when(top)
    def _():
        for m in range(MICRO):
            block = pl.ds(m * tb, tb)
            top_rows = (cot_v[block].astype(f32) * scale[m * tb : (m + 1) * tb]).astype(bf16)
            og[m] = top_rows
            slope = silu_slope(pre_v[block].astype(f32))
            top_gate[m] = (slope * top_rows.astype(f32)).astype(bf16)

    expected = 2 * CHIPS - 1 + CHIPS - 1 + LAYERS - 1
    expected = expected + jnp.where(s > 0, 1, 0) + jnp.where(top, 1, 0)
    pl.semaphore_wait(barrier, expected)

    turn = chip_of(c, z)
    plane_peers = [
        s * 16 + ((c // 4 + row) % 2 * 4 + (c + step) % 4) * 2 + k
        for row, step in ((1, 2), (0, 2), (1, 1), (1, 3), (0, 1), (0, 3), (1, 0))
    ]
    slots = [row * 4 + (z + step) % 4 for row, step in ROUTE]
    own_slot = slots[0]
    column_peers = [((z + i) % CHIPS, slots[i]) for i in (4, 3, 5, 2, 6, 1, 7)]

    @pl.when(top)
    def _():
        for m in range(MICRO):
            remote(top_gate.at[m], gates.at[m, k, turn], 0, turn_sem.at[m], device(s, turn, k, c))

    @pl.when(s < LAYERS - 1)
    def _():
        remote(pre_v, low_pre, 3, pre_sem.at[0], device(s + 1, c, k, z))

    for load in loads[2:]:
        load.wait()
    left = jnp.dot(in_v[...], left_v[...], preferred_element_type=f32)
    for h in range(2):
        sides[h, :, :half] = left[:, h * half : (h + 1) * half]
    for h in range(2):
        w_v[h] = w_v[h].T
    own_slope[...] = silu_slope(pre_v[...].astype(f32))

    @pl.when(s > 0)
    def _():
        arrived(low_pre, pre_sem.at[0])
        low_slope[...] = silu_slope(low_pre[...].astype(f32))

    def spread(m):
        mine = gates.at[m, k, c]
        arrived(mine, turn_sem.at[m])
        for peer in plane_peers:
            remote(mine, mine, 4, gate_sem.at[m], {"section": peer, "dp": z})

    def product(m, h):
        gate = gates[m, h].reshape(CHIPS * tb, cols)
        return jnp.dot(gate, w_v[h], preferred_element_type=f32)

    def exchange(m):
        arrived(gates.at[m, 0, : CHIPS - 1], gate_sem.at[m])
        remote(gates.at[m, k], gates.at[m, k], 5, core_sem.at[m], device(s, c, 1 - k, z))

        half_product[m] = product(m, k)

    def project(m):
        arrived(gates.at[m, 0], core_sem.at[m])
        total = half_product[m] + product(m, 1 - k)
        part_v[m] = total.astype(bf16).reshape(CHIPS, tb, cols)

        for t, slot in column_peers:
            remote(part_v.at[m, slot], parts.at[m, z], 6, part_sem.at[m],
                   {"section": position, "dp": t})
        parts[m, z] = part_v[m, own_slot]

    def wait_residual(m, which):
        @pl.when(which)
        def _():
            arrived(og.at[m], og_sem.at[m])

    def collect(m):
        wait_residual(m, (s > 0) & (s < LAYERS - 1))
        arrived(parts.at[m, : CHIPS - 1], part_sem.at[m])
        back = parts[m, 0].astype(f32)
        for i in range(1, CHIPS):
            back = back + parts[m, i].astype(f32)
        in_grad = (og[m].astype(f32) + back).astype(bf16)
        block = pl.ds(m * tb, tb)
        grads_ref[block] = in_grad

        @pl.when(s > 0)
        def _():
            next_gate[m] = (low_slope[block] * in_grad.astype(f32)).astype(bf16)
            ig[m] = in_grad
            remote(next_gate.at[m], gates.at[m, k, turn], 1, turn_sem.at[m],
                   device(s - 1, turn, k, c))
            remote(ig.at[m], og.at[m], 2, og_sem.at[m], device(s - 1, c, k, z))

    def score(step):
        if step == 0:
            for m in range(MICRO):
                wait_residual(m, s == 0)
            gate = (own_slope[...] * og[...].reshape(rows, cols).astype(f32)).astype(bf16)
            right = jnp.dot(gate, right_v[...], preferred_element_type=f32)
            for h in range(2):
                sides[h, :, half:] = right[:, h * half : (h + 1) * half]

            def send(i):
                c_, k_ = in_layer(i)
                eight = pl.ds(pl.multiple_of(c_ * 8, 8), 8)
                remote(sides.at[k_, eight], side_in.at[me], 7, score_sem.at[0],
                       device(s, c_, k_, z))

            each(1, 2 * CHIPS, send)
            side_in[me] = sides[k, pl.ds(pl.multiple_of(c * 8, 8), 8)]
        elif step == 1:
            arrived(side_in.at[: 2 * CHIPS - 1], score_sem.at[0])
            both = side_in[0]
            for i in range(1, 2 * CHIPS):
                both = both + side_in[i]
            product = both[:, :half] * both[:, half:]
            eight = lax.broadcasted_iota(jnp.int32, (8, half), 0)
            token = eight + c * 8
            one = jnp.sum(jnp.where(token < first, product, 0.0), axis=0, keepdims=True)
            later = (token >= first) & (token < first + second)
            two = jnp.sum(jnp.where(later, product, 0.0), axis=0, keepdims=True)
            per_row[...] = jnp.where(eight == 0, one, jnp.where(eight == 1, two, 0.0))
            each(1, 2 * CHIPS, lambda i: remote(
                per_row, row_in.at[me], 8, score_sem.at[1], device(s, *in_layer(i), z)))
            row_in[me] = per_row[...]
        elif step == 2:
            arrived(row_in.at[: 2 * CHIPS - 1], score_sem.at[1])
            for h in range(2):
                total = row_in[h]
                for i in range(1, CHIPS):
                    total = total + row_in[2 * i + h]
                layer_sum[:, h * half : (h + 1) * half] = total
            each(1, LAYERS, lambda i: remote(
                layer_sum, layer_in.at[s], 9, score_sem.at[2], device((s + i) % LAYERS, c, k, z)))
            layer_in[s] = layer_sum[...]
        else:
            arrived(layer_in.at[: LAYERS - 1], score_sem.at[2])
            total = layer_in[0]
            for i in range(1, LAYERS):
                total = total + layer_in[i]
            lane = lax.broadcasted_iota(jnp.int32, (2 * half, QUERIES), 0) // RANK
            query = lax.broadcasted_iota(jnp.int32, (2 * half, QUERIES), 1)
            pick = jnp.where(lane == query, 1.0, 0.0).astype(f32)
            summed = jnp.dot(total, pick, precision=lax.Precision.HIGHEST,
                             preferred_element_type=f32)
            scores_ref[...] = summed[: scores_ref.shape[0]]

    def early(step):
        @pl.when(s == 0)
        def _():
            score(step)

    def late(step):
        @pl.when(s > 0)
        def _():
            score(step)

    events = dict(s=spread, x=exchange, p=project, c=collect, r=score, e=early, l=late)
    for event, m in ORDER:
        events[event](m)

    @pl.when(top)
    def _():
        arrived(top_gate, send_sem.at[0])

    @pl.when(s > 0)
    def _():
        arrived(next_gate, send_sem.at[1])
        arrived(ig, send_sem.at[2])

    @pl.when(s < LAYERS - 1)
    def _():
        arrived(pre_v, send_sem.at[3])

    arrived(gates.at[:, 0, : CHIPS - 1], send_sem.at[4])
    arrived(gates.at[:, 0], send_sem.at[5])
    arrived(parts.at[:, : CHIPS - 1], send_sem.at[6])
    arrived(side_in.at[: 2 * CHIPS - 1], send_sem.at[7])
    arrived(row_in.at[: 2 * CHIPS - 1], send_sem.at[8])
    arrived(layer_in.at[: LAYERS - 1], send_sem.at[9])


def per_device(
    cotangent, lengths, example_ids, layer_inputs, preacts, weights, query_left, query_right
):
    rows, cols = preacts.shape
    tb = rows // MICRO
    width = QUERIES * RANK
    bf16, f32 = jnp.bfloat16, jnp.float32
    anywhere = pl.BlockSpec(memory_space=pl.ANY)
    in_vmem = pl.BlockSpec(memory_space=pltpu.VMEM)
    chunk = pltpu.VMEM((MICRO, tb, cols), bf16)
    block = pltpu.VMEM((rows, cols), bf16)
    sems = pltpu.SemaphoreType.DMA
    return pl.pallas_call(
        influence_kernel,
        out_shape=(
            jax.ShapeDtypeStruct((rows, cols), bf16),
            jax.ShapeDtypeStruct((lengths.shape[0], QUERIES), f32),
        ),
        in_specs=[pl.BlockSpec(memory_space=pltpu.SMEM)] + [anywhere] * 6,
        out_specs=(in_vmem, in_vmem),
        scratch_shapes=[
            block, block, block,
            pltpu.VMEM((2, cols, cols), bf16),
            pltpu.VMEM(query_left.shape, bf16),
            pltpu.VMEM(query_right.shape, bf16),
            block, pltpu.VMEM((rows, cols), f32), pltpu.VMEM((rows, cols), f32), chunk, chunk, chunk,
            pltpu.VMEM((MICRO, 2, CHIPS, tb, cols), bf16),
            pltpu.VMEM((MICRO, CHIPS * tb, cols), f32),
            pltpu.VMEM((MICRO, CHIPS, tb, cols), bf16),
            pltpu.VMEM((MICRO, CHIPS, tb, cols), bf16),
            chunk,
            pltpu.VMEM((2, rows, width), f32),
            pltpu.VMEM((2 * CHIPS, 8, width), f32),
            pltpu.VMEM((8, width // 2), f32),
            pltpu.VMEM((2 * CHIPS, 8, width // 2), f32),
            pltpu.VMEM((8, width), f32),
            pltpu.VMEM((LAYERS, 8, width), f32),
            sems((7,)), sems((1,)), sems((MICRO,)), sems((MICRO,)), sems((MICRO,)),
            sems((MICRO,)), sems((MICRO,)), sems((3,)), sems((10,)),
        ],
        compiler_params=pltpu.CompilerParams(collective_id=0, has_side_effects=True),
    )(lengths, cotangent, layer_inputs, preacts, weights, query_left, query_right)


def solution(mesh):
    placed = (
        P("dp", None),
        P("dp"),
        P("dp"),
        P("dp", "section"),
        P("dp", "section"),
        P("section", "dp"),
        P("section", None),
        P("section", None),
    )
    return jax.shard_map(
        per_device,
        mesh=mesh,
        in_specs=placed,
        out_specs=(P("dp", "section"), P("dp", None)),
        check_vma=False,
    )
```

```python
import jax
import jax.numpy as jnp
from jax import lax
from jax.experimental import pallas as pl
from jax.experimental.pallas import tpu as pltpu
from jax.sharding import PartitionSpec as P

LAYERS = 4
QUERIES = 16
RANK = 16
CHIPS = 8
MICRO = 8
MESH = pl.DeviceIdType.MESH
ORDER = (
    ("s", 0), ("s", 1), ("s", 2), ("s", 3), ("x", 0), ("p", 0), ("s", 4), ("x", 1), ("p", 1), ("s", 5), ("x", 2), ("p", 2), ("s", 6), ("x", 3), ("p", 3), ("s", 7), ("x", 4), ("e", 0), ("c", 0), ("p", 4), ("x", 5), ("c", 1), ("p", 5), ("x", 6), ("c", 2), ("p", 6), ("e", 1), ("x", 7), ("c", 3), ("p", 7), ("c", 4), ("c", 5), ("e", 2), ("c", 6), ("c", 7), ("l", 0), ("l", 1), ("l", 2), ("r", 3),
)
ROUTE = ((0, 2), (0, 3), (0, 0), (1, 3), (1, 0), (1, 1), (1, 2), (0, 1))


def silu_slope(preact):
    sigmoid_value = jax.nn.sigmoid(preact)
    return sigmoid_value * (1.0 + preact * (1.0 - sigmoid_value))


def looked_up(table, index):
    value = jnp.int32(table[0])
    for i in range(1, len(table)):
        value = jnp.where(index == i, table[i], value)
    return value


def chip_of(plane, source):
    away = (source + CHIPS - plane) % CHIPS
    row, step = (looked_up([pair[i] for pair in ROUTE], away) for i in range(2))
    return row * 4 + (plane + step) % 4


def source_of(plane, chip):
    away = [0] * CHIPS
    for i, (row, step) in enumerate(ROUTE):
        away[row * 4 + step] = i
    return (plane + looked_up(away, chip // 4 * 4 + (chip + 4 - plane % 4) % 4)) % CHIPS


def influence_kernel(
    lens_ref, cot_ref, in_ref, pre_ref, w_ref, left_ref, right_ref, grads_ref, scores_ref,
    cot_v, in_v, pre_v, w_v, left_v, right_v, low_pre, low_slope, own_slope, og, top_gate, next_gate, gates,
    half_product, part_v, parts, ig, sides, side_in, per_row, row_in, layer_sum, layer_in,
    load_sem, pre_sem, og_sem, turn_sem, gate_sem, core_sem, part_sem, score_sem, send_sem,
):
    position, z = lax.axis_index("section"), lax.axis_index("dp")
    s, c, k = position // 16, (position % 16) // 2, position % 2
    rows, cols = pre_v.shape
    tb = rows // MICRO
    half = QUERIES * RANK // 2
    top = s == LAYERS - 1
    f32, bf16 = jnp.float32, jnp.bfloat16
    me = c * 2 + k

    def device(s_, c_, k_, z_):
        return {"section": s_ * 16 + c_ * 2 + k_, "dp": z_}

    def in_layer(i):
        return (c + i // 2) % CHIPS, (k + i % 2) % 2

    def remote(src, dst, phase, sem, where):
        pltpu.make_async_remote_copy(
            src_ref=src, dst_ref=dst, send_sem=send_sem.at[phase], recv_sem=sem,
            device_id=where, device_id_type=MESH,
        ).start()

    def arrived(ref, sem):
        pltpu.make_async_copy(ref, ref, sem).wait()

    def each(first, last, body):
        def step(i, carry):
            body(i)
            return carry

        lax.fori_loop(first, last, step, 0)

    first_col = pl.multiple_of(me * cols, cols)
    loads = [
        pltpu.make_async_copy(cot_ref.at[:, pl.ds(first_col, cols)], cot_v, load_sem.at[0]),
        pltpu.make_async_copy(pre_ref, pre_v, load_sem.at[1]),
        pltpu.make_async_copy(w_ref.at[:, pl.ds(0, cols)], w_v.at[0], load_sem.at[2]),
        pltpu.make_async_copy(w_ref.at[:, pl.ds(cols, cols)], w_v.at[1], load_sem.at[3]),
        pltpu.make_async_copy(in_ref, in_v, load_sem.at[4]),
        pltpu.make_async_copy(left_ref, left_v, load_sem.at[5]),
        pltpu.make_async_copy(right_ref, right_v, load_sem.at[6]),
    ]
    for load in loads:
        load.start()

    barrier = pltpu.get_barrier_semaphore()

    def greet(where):
        pl.semaphore_signal(barrier, inc=1, device_id=where, device_id_type=MESH)

    greet(device(jnp.minimum(s + 1, LAYERS - 1), z, k, source_of(z, c)))
    each(1, LAYERS, lambda i: greet(device((s + i) % LAYERS, c, k, z)))
    each(1, CHIPS, lambda i: greet(device(s, c, k, (z + i) % CHIPS)))
    each(1, 2 * CHIPS, lambda i: greet(device(s, *in_layer(i), z)))

    first, second = lens_ref[0], lens_ref[1]
    row = lax.broadcasted_iota(jnp.int32, (rows, 1), 0)
    count = jnp.where(row < first, first, second).astype(f32)
    scale = jnp.where(row < first + second, 1.0 / jnp.maximum(count, 1.0), 0.0)
    loads[0].wait()
    loads[1].wait()

    @pl.when(top)
    def _():
        for m in range(MICRO):
            block = pl.ds(m * tb, tb)
            top_rows = (cot_v[block].astype(f32) * scale[m * tb : (m + 1) * tb]).astype(bf16)
            og[m] = top_rows
            slope = silu_slope(pre_v[block].astype(f32))
            top_gate[m] = (slope * top_rows.astype(f32)).astype(bf16)

    expected = 2 * CHIPS - 1 + CHIPS - 1 + LAYERS - 1
    expected = expected + jnp.where(s > 0, 1, 0) + jnp.where(top, 1, 0)
    pl.semaphore_wait(barrier, expected)

    turn = chip_of(c, z)
    plane_peers = [
        s * 16 + ((c // 4 + row) % 2 * 4 + (c + step) % 4) * 2 + k
        for row, step in ((1, 2), (0, 2), (1, 1), (1, 3), (0, 1), (0, 3), (1, 0))
    ]
    slots = [row * 4 + (z + step) % 4 for row, step in ROUTE]
    own_slot = slots[0]
    column_peers = [((z + i) % CHIPS, slots[i]) for i in (4, 3, 5, 2, 6, 1, 7)]

    @pl.when(top)
    def _():
        for m in range(MICRO):
            remote(top_gate.at[m], gates.at[m, k, turn], 0, turn_sem.at[m], device(s, turn, k, c))

    @pl.when(s < LAYERS - 1)
    def _():
        remote(pre_v, low_pre, 3, pre_sem.at[0], device(s + 1, c, k, z))

    for load in loads[2:]:
        load.wait()
    left = jnp.dot(in_v[...], left_v[...], preferred_element_type=f32)
    for h in range(2):
        sides[h, :, :half] = left[:, h * half : (h + 1) * half]
    for h in range(2):
        w_v[h] = w_v[h].T
    own_slope[...] = silu_slope(pre_v[...].astype(f32))

    @pl.when(s > 0)
    def _():
        arrived(low_pre, pre_sem.at[0])
        low_slope[...] = silu_slope(low_pre[...].astype(f32))

    def spread(m):
        mine = gates.at[m, k, c]
        arrived(mine, turn_sem.at[m])
        for peer in plane_peers:
            remote(mine, mine, 4, gate_sem.at[m], {"section": peer, "dp": z})

    def product(m, h):
        gate = gates[m, h].reshape(CHIPS * tb, cols)
        return jnp.dot(gate, w_v[h], preferred_element_type=f32)

    def exchange(m):
        arrived(gates.at[m, 0, : CHIPS - 1], gate_sem.at[m])
        remote(gates.at[m, k], gates.at[m, k], 5, core_sem.at[m], device(s, c, 1 - k, z))

        half_product[m] = product(m, k)

    def project(m):
        arrived(gates.at[m, 0], core_sem.at[m])
        total = half_product[m] + product(m, 1 - k)
        part_v[m] = total.astype(bf16).reshape(CHIPS, tb, cols)

        for t, slot in column_peers:
            remote(part_v.at[m, slot], parts.at[m, z], 6, part_sem.at[m],
                   {"section": position, "dp": t})
        parts[m, z] = part_v[m, own_slot]

    def wait_residual(m, which):
        @pl.when(which)
        def _():
            arrived(og.at[m], og_sem.at[m])

    def collect(m):
        wait_residual(m, (s > 0) & (s < LAYERS - 1))
        arrived(parts.at[m, : CHIPS - 1], part_sem.at[m])
        back = parts[m, 0].astype(f32)
        for i in range(1, CHIPS):
            back = back + parts[m, i].astype(f32)
        in_grad = (og[m].astype(f32) + back).astype(bf16)
        block = pl.ds(m * tb, tb)
        grads_ref[block] = in_grad

        @pl.when(s > 0)
        def _():
            next_gate[m] = (low_slope[block] * in_grad.astype(f32)).astype(bf16)
            ig[m] = in_grad
            remote(next_gate.at[m], gates.at[m, k, turn], 1, turn_sem.at[m],
                   device(s - 1, turn, k, c))
            remote(ig.at[m], og.at[m], 2, og_sem.at[m], device(s - 1, c, k, z))

    def score(step):
        if step == 0:
            for m in range(MICRO):
                wait_residual(m, s == 0)
            gate = (own_slope[...] * og[...].reshape(rows, cols).astype(f32)).astype(bf16)
            right = jnp.dot(gate, right_v[...], preferred_element_type=f32)
            for h in range(2):
                sides[h, :, half:] = right[:, h * half : (h + 1) * half]

            def send(i):
                c_, k_ = in_layer(i)
                eight = pl.ds(pl.multiple_of(c_ * 8, 8), 8)
                remote(sides.at[k_, eight], side_in.at[me], 7, score_sem.at[0],
                       device(s, c_, k_, z))

            each(1, 2 * CHIPS, send)
            side_in[me] = sides[k, pl.ds(pl.multiple_of(c * 8, 8), 8)]
        elif step == 1:
            arrived(side_in.at[: 2 * CHIPS - 1], score_sem.at[0])
            both = side_in[0]
            for i in range(1, 2 * CHIPS):
                both = both + side_in[i]
            product = both[:, :half] * both[:, half:]
            eight = lax.broadcasted_iota(jnp.int32, (8, half), 0)
            token = eight + c * 8
            one = jnp.sum(jnp.where(token < first, product, 0.0), axis=0, keepdims=True)
            later = (token >= first) & (token < first + second)
            two = jnp.sum(jnp.where(later, product, 0.0), axis=0, keepdims=True)
            per_row[...] = jnp.where(eight == 0, one, jnp.where(eight == 1, two, 0.0))
            each(1, 2 * CHIPS, lambda i: remote(
                per_row, row_in.at[me], 8, score_sem.at[1], device(s, *in_layer(i), z)))
            row_in[me] = per_row[...]
        elif step == 2:
            arrived(row_in.at[: 2 * CHIPS - 1], score_sem.at[1])
            for h in range(2):
                total = row_in[h]
                for i in range(1, CHIPS):
                    total = total + row_in[2 * i + h]
                layer_sum[:, h * half : (h + 1) * half] = total
            each(1, LAYERS, lambda i: remote(
                layer_sum, layer_in.at[s], 9, score_sem.at[2], device((s + i) % LAYERS, c, k, z)))
            layer_in[s] = layer_sum[...]
        else:
            arrived(layer_in.at[: LAYERS - 1], score_sem.at[2])
            total = layer_in[0]
            for i in range(1, LAYERS):
                total = total + layer_in[i]
            lane = lax.broadcasted_iota(jnp.int32, (2 * half, QUERIES), 0) // RANK
            query = lax.broadcasted_iota(jnp.int32, (2 * half, QUERIES), 1)
            pick = jnp.where(lane == query, 1.0, 0.0).astype(f32)
            summed = jnp.dot(total, pick, precision=lax.Precision.HIGHEST,
                             preferred_element_type=f32)
            scores_ref[...] = summed[: scores_ref.shape[0]]

    def early(step):
        @pl.when(s == 0)
        def _():
            score(step)

    def late(step):
        @pl.when(s > 0)
        def _():
            score(step)

    events = dict(s=spread, x=exchange, p=project, c=collect, r=score, e=early, l=late)
    for event, m in ORDER:
        events[event](m)

    @pl.when(top)
    def _():
        arrived(top_gate, send_sem.at[0])

    @pl.when(s > 0)
    def _():
        arrived(next_gate, send_sem.at[1])
        arrived(ig, send_sem.at[2])

    @pl.when(s < LAYERS - 1)
    def _():
        arrived(pre_v, send_sem.at[3])

    arrived(gates.at[:, 0, : CHIPS - 1], send_sem.at[4])
    arrived(gates.at[:, 0], send_sem.at[5])
    arrived(parts.at[:, : CHIPS - 1], send_sem.at[6])
    arrived(side_in.at[: 2 * CHIPS - 1], send_sem.at[7])
    arrived(row_in.at[: 2 * CHIPS - 1], send_sem.at[8])
    arrived(layer_in.at[: LAYERS - 1], send_sem.at[9])


def per_device(
    cotangent, lengths, example_ids, layer_inputs, preacts, weights, query_left, query_right
):
    rows, cols = preacts.shape
    tb = rows // MICRO
    width = QUERIES * RANK
    bf16, f32 = jnp.bfloat16, jnp.float32
    anywhere = pl.BlockSpec(memory_space=pl.ANY)
    in_vmem = pl.BlockSpec(memory_space=pltpu.VMEM)
    chunk = pltpu.VMEM((MICRO, tb, cols), bf16)
    block = pltpu.VMEM((rows, cols), bf16)
    sems = pltpu.SemaphoreType.DMA
    return pl.pallas_call(
        influence_kernel,
        out_shape=(
            jax.ShapeDtypeStruct((rows, cols), bf16),
            jax.ShapeDtypeStruct((lengths.shape[0], QUERIES), f32),
        ),
        in_specs=[pl.BlockSpec(memory_space=pltpu.SMEM)] + [anywhere] * 6,
        out_specs=(in_vmem, in_vmem),
        scratch_shapes=[
            block, block, block,
            pltpu.VMEM((2, cols, cols), bf16),
            pltpu.VMEM(query_left.shape, bf16),
            pltpu.VMEM(query_right.shape, bf16),
            block, pltpu.VMEM((rows, cols), f32), pltpu.VMEM((rows, cols), f32), chunk, chunk, chunk,
            pltpu.VMEM((MICRO, 2, CHIPS, tb, cols), bf16),
            pltpu.VMEM((MICRO, CHIPS * tb, cols), f32),
            pltpu.VMEM((MICRO, CHIPS, tb, cols), bf16),
            pltpu.VMEM((MICRO, CHIPS, tb, cols), bf16),
            chunk,
            pltpu.VMEM((2, rows, width), f32),
            pltpu.VMEM((2 * CHIPS, 8, width), f32),
            pltpu.VMEM((8, width // 2), f32),
            pltpu.VMEM((2 * CHIPS, 8, width // 2), f32),
            pltpu.VMEM((8, width), f32),
            pltpu.VMEM((LAYERS, 8, width), f32),
            sems((7,)), sems((1,)), sems((MICRO,)), sems((MICRO,)), sems((MICRO,)),
            sems((MICRO,)), sems((MICRO,)), sems((3,)), sems((10,)),
        ],
        compiler_params=pltpu.CompilerParams(collective_id=0, has_side_effects=True),
    )(lengths, cotangent, layer_inputs, preacts, weights, query_left, query_right)


def solution(mesh):
    placed = (
        P("dp", None),
        P("dp"),
        P("dp"),
        P("dp", "section"),
        P("dp", "section"),
        P("section", "dp"),
        P("section", None),
        P("section", None),
    )
    return jax.shard_map(
        per_device,
        mesh=mesh,
        in_specs=placed,
        out_specs=(P("dp", "section"), P("dp", None)),
        check_vma=False,
    )
```
